32 devices in a mesh: grp: 4 (over x, core), var: 8 (over z, y).
Axes of the slice: x: 2, y: 2, z: 4, core: 2. Of those that a mesh axis runs over, the one named last changes fastest.
Arguments:
- dosages: int32 [16384, 8192], P('grp', 'var'), may hold values from 0 to 2
- variant_weight: bfloat16 [8192], P('var'), may hold values from -2 to 2
- block_id: int32 [8192], P('var'), may hold values from 0 to 127
- stack_weight: bfloat16 [1024, 64], replicated, may hold values from -0.1875 to 0.1875
- labels: int32 [16384, 64], P(('grp', 'var')), may hold values 0 or 1
Outputs:
- level_grad: float32 [1024, 64], P('var')
- weight_grad: float32 [8192], P('var')
The draws below stay inside these ranges and needn't reach their ends.
All inputs are finite; a program needn't handle non-finite values. No bound on the sum of `labels` on one device may be relied on, other than what follows from the above.
Results may differ from the reference program's by a relative error of at most 0.00039.
Values may be sent and summed in bfloat16 or wider, within the bound.
A program may use at most 64 MiB of HBM per device.

```python
import math
import jax
import jax.numpy as jnp
from jax import lax

M_DEV = 1024
KB = 128
TRAITS = 64
PERSONS = 16384
M = 8192
K = 1024
N_VAR = 8


def with_ends(result, own_key, smallest, largest):
    place = [jax.random.randint(jax.random.fold_in(own_key, axis), (), 0, length) for axis, length in enumerate(result.shape)]
    main_axis = result.shape.index(max(result.shape))
    neighbour = place[:main_axis] + [(place[main_axis] + 1) % result.shape[main_axis]] + place[main_axis + 1:]
    return result.at[tuple(place)].set(smallest).at[tuple(neighbour)].set(largest)


def levels(key, shape, split, smallest, largest):
    def one(position, blocks):
        steps = jax.random.uniform(jax.random.fold_in(jax.random.fold_in(key, 6), position), (blocks,), jnp.float32, smallest / len(split), largest / len(split))
        return jnp.repeat(jnp.exp(steps), shape[position] // blocks).reshape((-1,) + (1,) * (len(shape) - position - 1))

    level = one(*split[0])
    for cut in split[1:]:
        level = level * one(*cut)
    return level


def gaussian(key, dims, scale, bound, pieces=(), kind=jnp.bfloat16):
    array = jax.random.normal(key, dims, jnp.float32) * scale
    if len(pieces) > 0:
        array = levels(key, dims, pieces, -0.22, 0.18) * array
    return jnp.clip(array, min=-bound, max=bound).astype(kind)


def setup_inputs(seed: int = 0) -> dict:
    arg_keys = jax.random.split(jax.random.key(seed), 6)
    dosages = with_ends(jax.random.randint(arg_keys[0], (PERSONS, M), 0, 3), jax.random.fold_in(arg_keys[0], 1), 0, 2).astype(jnp.int32)
    variant_weight = gaussian(arg_keys[1], (M,), (M_DEV // KB) ** -0.5, 2.0, ((0, 8),))
    block_id = with_ends(jax.random.randint(arg_keys[2], (M,), 0, KB), jax.random.fold_in(arg_keys[2], 1), 0, KB - 1).astype(jnp.int32)
    stack_weight = gaussian(arg_keys[3], (K, TRAITS), K ** -0.5, 0.1875)
    labels = with_ends((jax.random.randint(arg_keys[4], (PERSONS, TRAITS), 0, 2) < 1).astype(jnp.int32), jax.random.fold_in(arg_keys[4], 1), 0, 1)
    return {"dosages": dosages, "variant_weight": variant_weight, "block_id": block_id, "stack_weight": stack_weight, "labels": labels}


def reference(dosages, variant_weight, block_id, stack_weight, labels):
    norm_scale = 1.0 / math.sqrt(PERSONS)
    shard_ids = jnp.arange(N_VAR, dtype=jnp.int32)

    def make_block(shard):
        start = (shard * M_DEV).astype(jnp.int32)
        dose_part = lax.dynamic_slice_in_dim(dosages, start, M_DEV, 1).astype(jnp.float32)
        weight_part = lax.dynamic_slice_in_dim(variant_weight, start, M_DEV, 0).astype(jnp.float32)
        block_part = lax.dynamic_slice_in_dim(block_id, start, M_DEV, 0)
        product = dose_part * weight_part[None, :]
        summed = jax.ops.segment_sum(product.T, block_part, num_segments=KB)
        return summed.T.astype(jnp.bfloat16)
    blocks = lax.map(make_block, shard_ids)
    predictors = jnp.transpose(blocks, (1, 0, 2)).reshape(PERSONS, K)
    logits = jnp.dot(predictors, stack_weight, preferred_element_type=jnp.float32)
    resid = (jax.nn.sigmoid(logits) - labels.astype(jnp.float32)).astype(jnp.bfloat16)
    level_grad = jnp.dot(predictors.T, resid, preferred_element_type=jnp.float32) * norm_scale
    pred_grad = jnp.dot(resid, stack_weight.T, preferred_element_type=jnp.float32).astype(jnp.bfloat16)

    def weight_block(shard):
        start = (shard * M_DEV).astype(jnp.int32)
        dose_part = lax.dynamic_slice_in_dim(dosages, start, M_DEV, 1).astype(jnp.float32)
        block_part = lax.dynamic_slice_in_dim(block_id, start, M_DEV, 0)
        grad_part = lax.dynamic_slice_in_dim(pred_grad, (shard * KB).astype(jnp.int32), KB, 1)
        picked = jnp.take(grad_part, block_part, axis=1).astype(jnp.float32)
        return lax.optimization_barrier(jnp.sum(dose_part * picked, axis=0)) * norm_scale
    weight_grad = lax.map(weight_block, shard_ids).reshape(M)
    return (level_grad, weight_grad)
```

```python
import functools
import math

import jax
import jax.numpy as jnp
from jax import lax
from jax.experimental import pallas as pl
from jax.experimental.pallas import tpu as pltpu
from jax.sharding import PartitionSpec as P

F32, BF16 = jnp.float32, jnp.bfloat16


def flip(a, k, count):
    total, bit = 0, 1
    while bit < count:
        total = total + bit * ((a // bit + k // bit) % 2)
        bit *= 2
    return total


def kernel(
    nvar, ngrp, norm, dos, wt, bid, sw, lab, lev_out, wg_out,
    dint, dose, wmat, bd, wown, labv, pred, part, own, yrecv, ysum, zrecv, gathz, gathy,
    colacc, levacc, redl, redw,
    dsem, csem, ys, yr, zs, zr, gzs, gzr, gys, gyr, rs, rr,
):
    nz = nvar // 2
    rows = labv.shape[0]
    half = rows // 2
    kb, traits = wown.shape
    v = lax.axis_index("var")
    g = lax.axis_index("grp")
    z, y = v // 2, v % 2
    partner = z * 2 + (1 - y)

    def block_of(i, parity):
        return flip(z, nz - 1 - i, nz) * 2 + parity

    def dose_copy(s, b):
        start = pl.multiple_of(b * rows, rows)
        return pltpu.make_async_copy(dos.at[pl.ds(start, rows)], dint.at[s], dsem.at[s])

    sw_copy = pltpu.make_async_copy(sw.at[pl.ds(pl.multiple_of(v * kb, kb), kb)], wown, csem.at[0])
    lab_copy = pltpu.make_async_copy(lab, labv, csem.at[1])
    sw_copy.start()
    for i in range(nz):
        dose_copy(i, block_of(i, 1 - y)).start()
    for i in range(nz):
        dose_copy(nz + i, block_of(i, y)).start()
    lab_copy.start()

    barrier = pltpu.get_barrier_semaphore()
    pl.semaphore_signal(barrier, inc=1, device_id={"var": partner})
    for i in range(nz - 1):
        pl.semaphore_signal(barrier, inc=1, device_id={"var": block_of(i, y)})
    for d in range(1, ngrp):
        pl.semaphore_signal(barrier, inc=1, device_id={"grp": (g + d) % ngrp})

    hot = lax.broadcasted_iota(jnp.int32, (kb, wt.shape[1]), 0) == bid[...]
    wmat[...] = jnp.where(hot, wt[...].astype(F32), 0.0).T.astype(BF16)
    sw_copy.wait()
    w = wown[...].astype(F32)
    zero = jnp.zeros_like(w)
    bd[0:kb, :] = jnp.concatenate([w, zero], axis=1).astype(BF16)
    bd[kb : 2 * kb, :] = jnp.concatenate([zero, w], axis=1).astype(BF16)
    colacc[...] = jnp.zeros_like(colacc)
    levacc[...] = jnp.zeros_like(levacc)

    def forward(s, b):
        dose_copy(s, b).wait()
        d = dint[s].astype(F32).astype(BF16)
        dose[b] = d
        p = jnp.dot(d, wmat[...], preferred_element_type=F32).astype(BF16)
        pp = jnp.concatenate([p[:half], p[half:]], axis=1)
        pred[b] = pp
        return jnp.dot(pp, bd[...], preferred_element_type=F32)

    def y_copy(i):
        return pltpu.make_async_remote_copy(
            part.at[i], yrecv.at[i], ys.at[i], yr.at[i], device_id={"var": partner}
        )

    def z_copy(i):
        return pltpu.make_async_remote_copy(
            ysum.at[i], zrecv.at[i], zs.at[i], zr.at[i], device_id={"var": block_of(i, y)}
        )

    def gz_copy(i):
        return pltpu.make_async_remote_copy(
            gathz.at[nz - 1], gathz.at[i], gzs.at[i], gzr.at[i], device_id={"var": block_of(i, y)}
        )

    def gy_copy(i):
        return pltpu.make_async_remote_copy(
            gathz.at[i], gathy.at[i], gys.at[i], gyr.at[i], device_id={"var": partner}
        )

    part[0] = forward(0, block_of(0, 1 - y))
    pl.semaphore_wait(barrier, nz + ngrp - 1)
    y_copy(0).start()

    def first(i, carry):
        part[i] = forward(i, block_of(i, 1 - y))
        y_copy(i).start()
        return carry

    lax.fori_loop(1, nz, first, 0)

    def second(i, carry):
        own[i] = forward(nz + i, block_of(i, y))
        return carry

    lax.fori_loop(0, nz, second, 0)

    lab_copy.wait()
    target = labv[...].astype(F32)
    target = jnp.concatenate([target[:half], target[half:]], axis=1)

    for i in range(nz - 1):
        y_copy(i).wait_recv()
        ysum[i] = own[i] + yrecv[i]
        z_copy(i).start()
    y_copy(nz - 1).wait_recv()
    logits = own[nz - 1] + yrecv[nz - 1]
    for i in range(nz - 1):
        z_copy(i).wait_recv()
        logits = logits + zrecv[i]
    gathz[nz - 1] = (jax.nn.sigmoid(logits) - target).astype(BF16)
    for i in range(nz - 1):
        gz_copy(i).start()
    gy_copy(nz - 1).start()

    def backward(resid, b):
        lg = lax.dot_general(
            resid, bd[...], (((1,), (1,)), ((), ())), preferred_element_type=F32
        ).astype(BF16)
        lg = jnp.concatenate([lg[:, :kb], lg[:, kb:]], axis=0)
        colacc[...] += lax.dot_general(
            lg, dose[b], (((0,), (0,)), ((), ())), preferred_element_type=F32
        )
        levacc[...] += lax.dot_general(
            pred[b], resid, (((0,), (0,)), ((), ())), preferred_element_type=F32
        )

    backward(gathz[nz - 1], v)
    gy_copy(nz - 1).wait_recv()
    backward(gathy[nz - 1], partner)

    def gather_z(i, carry):
        gz_copy(i).wait_recv()
        gy_copy(i).start()
        backward(gathz[i], block_of(i, y))
        return carry

    lax.fori_loop(0, nz - 1, gather_z, 0)

    def gather_y(i, carry):
        gy_copy(i).wait_recv()
        backward(gathy[i], block_of(i, 1 - y))
        return carry

    lax.fori_loop(0, nz - 1, gather_y, 0)

    hot = lax.broadcasted_iota(jnp.int32, colacc.shape, 0) == bid[...]
    redw[g] = jnp.sum(jnp.where(hot, colacc[...], 0.0), axis=0, keepdims=True)
    lev = levacc[0:kb, 0:traits] + levacc[kb : 2 * kb, traits : 2 * traits]
    redl[g] = jnp.concatenate([lev[: kb // 2], lev[kb // 2 :]], axis=1)

    def r_copies(d):
        peer = {"grp": (g + d) % ngrp}
        return (
            pltpu.make_async_remote_copy(
                redl.at[g], redl.at[g], rs.at[0, d - 1], rr.at[0, d - 1], device_id=peer
            ),
            pltpu.make_async_remote_copy(
                redw.at[g], redw.at[g], rs.at[1, d - 1], rr.at[1, d - 1], device_id=peer
            ),
        )

    for d in range(1, ngrp):
        for copy in r_copies(d):
            copy.start()
    for d in range(1, ngrp):
        for copy in r_copies(d):
            copy.wait_recv()
    total, weight = redl[0], redw[0]
    for e in range(1, ngrp):
        total = total + redl[e]
        weight = weight + redw[e]
    total = total * norm
    lev_out[0 : kb // 2, :] = total[:, :traits]
    lev_out[kb // 2 : kb, :] = total[:, traits:]
    wg_out[...] = weight * norm

    for i in range(nz):
        y_copy(i).wait_send()
        gy_copy(i).wait_send()
    for i in range(nz - 1):
        z_copy(i).wait_send()
        gz_copy(i).wait_send()
    for d in range(1, ngrp):
        for copy in r_copies(d):
            copy.wait_send()


def local(dosages, variant_weight, block_id, stack_weight, labels):
    persons, variants = dosages.shape
    nvar, ngrp = lax.axis_size("var"), lax.axis_size("grp")
    total_preds, traits = stack_weight.shape
    kb = total_preds // nvar
    rows = labels.shape[0]
    half, nz = rows // 2, nvar // 2
    norm = 1.0 / math.sqrt(persons * ngrp)
    block = (half, 2 * traits)
    dma = pltpu.SemaphoreType.DMA
    hbm = pl.BlockSpec(memory_space=pl.ANY)
    vmem = pl.BlockSpec(memory_space=pltpu.VMEM)
    level, weight = pl.pallas_call(
        functools.partial(kernel, nvar, ngrp, norm),
        out_shape=(
            jax.ShapeDtypeStruct((kb, traits), F32),
            jax.ShapeDtypeStruct((1, variants), F32),
        ),
        in_specs=[hbm, vmem, vmem, hbm, hbm],
        out_specs=(vmem, vmem),
        scratch_shapes=[
            pltpu.VMEM((nvar, rows, variants), jnp.int32),
            pltpu.VMEM((nvar, rows, variants), BF16),
            pltpu.VMEM((variants, kb), BF16),
            pltpu.VMEM((2 * kb, 2 * traits), BF16),
            pltpu.VMEM((kb, traits), BF16),
            pltpu.VMEM((rows, traits), jnp.int32),
            pltpu.VMEM((nvar, half, 2 * kb), BF16),
            pltpu.VMEM((nz,) + block, F32),
            pltpu.VMEM((nz,) + block, F32),
            pltpu.VMEM((nz,) + block, F32),
            pltpu.VMEM((nz,) + block, F32),
            pltpu.VMEM((nz,) + block, F32),
            pltpu.VMEM((nz,) + block, BF16),
            pltpu.VMEM((nz,) + block, BF16),
            pltpu.VMEM((kb, variants), F32),
            pltpu.VMEM((2 * kb, 2 * traits), F32),
            pltpu.VMEM((ngrp, kb // 2, 2 * traits), F32),
            pltpu.VMEM((ngrp, 1, variants), F32),
            dma((nvar,)),
            dma((2,)),
            dma((nz,)),
            dma((nz,)),
            dma((nz,)),
            dma((nz,)),
            dma((nz,)),
            dma((nz,)),
            dma((nz,)),
            dma((nz,)),
            dma((2, ngrp - 1)),
            dma((2, ngrp - 1)),
        ],
        compiler_params=pltpu.CompilerParams(
            collective_id=0, has_side_effects=True, vmem_limit_bytes=60 * 1024 * 1024
        ),
    )(dosages, variant_weight[None, :], block_id[None, :], stack_weight, labels)
    return level, weight.reshape(variants)


def solution(mesh):
    return jax.shard_map(
        local,
        mesh=mesh,
        in_specs=(P("grp", "var"), P("var"), P("var"), P(), P(("grp", "var"), None)),
        out_specs=(P("var", None), P("var")),
        check_vma=False,
    )
```

```python
import functools
import math

import jax
import jax.numpy as jnp
from jax import lax
from jax.experimental import pallas as pl
from jax.experimental.pallas import tpu as pltpu
from jax.sharding import PartitionSpec as P

F32, BF16 = jnp.float32, jnp.bfloat16


def flip(a, k, count):
    total, bit = 0, 1
    while bit < count:
        total = total + bit * ((a // bit + k // bit) % 2)
        bit *= 2
    return total


def kernel(
    nvar, ngrp, dos, wt_hbm, bid_hbm, sw, lab, redl, redw,
    wt, bid, dint, dose, wmat, wback, wown, labv, pred, part, own, yrecv, ysum, zrecv, gathz, gathy,
    colacc, levacc,
    dsem, csem, ys, yr, zs, zr, gzs, gzr, gys, gyr, rs, rr,
):
    nz = nvar // 2
    rows = labv.shape[1]
    traits, kb = wown.shape
    v = lax.axis_index("var")
    g = lax.axis_index("grp")
    z, y = v // 2, v % 2
    partner = z * 2 + (1 - y)

    def block_of(i, parity):
        return flip(z, nz - 1 - i, nz) * 2 + parity

    def dose_copy(s, b):
        start = pl.multiple_of(b * rows, rows)
        return pltpu.make_async_copy(dos.at[pl.ds(start, rows)], dint.at[s], dsem.at[s])

    sw_copy = pltpu.make_async_copy(sw.at[:, pl.ds(pl.multiple_of(v * kb, kb), kb)], wown, csem.at[0])
    lab_copy = pltpu.make_async_copy(lab, labv, csem.at[1])
    wt_copy = pltpu.make_async_copy(wt_hbm, wt, csem.at[2])
    bid_copy = pltpu.make_async_copy(bid_hbm, bid, csem.at[3])
    wt_copy.start()
    bid_copy.start()
    sw_copy.start()
    for i in range(nz):
        dose_copy(i, block_of(i, 1 - y)).start()
    for i in range(nz):
        dose_copy(nz + i, block_of(i, y)).start()
    lab_copy.start()

    barrier = pltpu.get_barrier_semaphore()
    pl.semaphore_signal(barrier, inc=1, device_id={"var": partner})
    for i in range(nz - 1):
        pl.semaphore_signal(barrier, inc=1, device_id={"var": block_of(i, y)})
    for d in range(1, ngrp):
        pl.semaphore_signal(barrier, inc=1, device_id={"grp": (g + d) % ngrp})

    wt_copy.wait()
    bid_copy.wait()
    hot = lax.broadcasted_iota(jnp.int32, (kb, wt.shape[0]), 0) == bid[...][None, :]
    wmat[...] = jnp.where(hot, wt[...].astype(F32)[None, :], 0.0).T.astype(BF16)
    sw_copy.wait()
    wback[...] = wown[...].astype(F32).T.astype(BF16)
    colacc[...] = jnp.zeros_like(colacc)
    levacc[...] = jnp.zeros_like(levacc)

    def forward(s, b):
        dose_copy(s, b).wait()
        d = dint[s].astype(F32).astype(BF16)
        dose[b] = d
        p = jnp.dot(d, wmat[...], preferred_element_type=F32).astype(BF16)
        pred[b] = p
        return lax.dot_general(
            wown[...], p, (((1,), (1,)), ((), ())), preferred_element_type=F32
        )

    def y_copy(i):
        return pltpu.make_async_remote_copy(
            part.at[i], yrecv.at[i], ys.at[i], yr.at[i], device_id={"var": partner}
        )

    def z_copy(i):
        return pltpu.make_async_remote_copy(
            ysum.at[i], zrecv.at[i], zs.at[i], zr.at[i], device_id={"var": block_of(i, y)}
        )

    def gz_copy(i):
        return pltpu.make_async_remote_copy(
            gathz.at[nz - 1], gathz.at[i], gzs.at[i], gzr.at[i], device_id={"var": block_of(i, y)}
        )

    def gy_copy(i):
        return pltpu.make_async_remote_copy(
            gathz.at[i], gathy.at[i], gys.at[i], gyr.at[i], device_id={"var": partner}
        )

    part[0] = forward(0, block_of(0, 1 - y))
    pl.semaphore_wait(barrier, nz + ngrp - 1)
    y_copy(0).start()

    def first(i, carry):
        part[i] = forward(i, block_of(i, 1 - y))
        y_copy(i).start()
        return carry

    lax.fori_loop(1, nz, first, 0)

    def second(i, carry):
        own[i] = forward(nz + i, block_of(i, y))
        return carry

    lax.fori_loop(0, nz, second, 0)

    lab_copy.wait()
    target = labv[...].astype(F32)

    for i in range(nz - 1):
        y_copy(i).wait_recv()
        ysum[i] = own[i] + yrecv[i]
        z_copy(i).start()
    y_copy(nz - 1).wait_recv()
    logits = own[nz - 1] + yrecv[nz - 1]
    for i in range(nz - 1):
        z_copy(i).wait_recv()
        logits = logits + zrecv[i]
    gathz[nz - 1] = (jax.nn.sigmoid(logits) - target).astype(BF16)
    for i in range(nz - 1):
        gz_copy(i).start()
    gy_copy(nz - 1).start()

    def backward(resid, b):
        lg = jnp.dot(wback[...], resid, preferred_element_type=F32).astype(BF16)
        colacc[...] += jnp.dot(lg, dose[b], preferred_element_type=F32)
        levacc[...] += jnp.dot(resid, pred[b], preferred_element_type=F32)

    backward(gathz[nz - 1], v)
    gy_copy(nz - 1).wait_recv()
    backward(gathy[nz - 1], partner)

    def gather_z(i, carry):
        gz_copy(i).wait_recv()
        gy_copy(i).start()
        backward(gathz[i], block_of(i, y))
        return carry

    lax.fori_loop(0, nz - 1, gather_z, 0)

    def gather_y(i, carry):
        gy_copy(i).wait_recv()
        backward(gathy[i], block_of(i, 1 - y))
        return carry

    lax.fori_loop(0, nz - 1, gather_y, 0)

    hot = lax.broadcasted_iota(jnp.int32, colacc.shape, 0) == bid[...][None, :]
    redw[g] = jnp.sum(jnp.where(hot, colacc[...], 0.0), axis=0, keepdims=True)
    redl[g] = levacc[...]

    def r_copies(d):
        peer = {"grp": (g + d) % ngrp}
        return (
            pltpu.make_async_remote_copy(
                redl.at[g], redl.at[g], rs.at[0, d - 1], rr.at[0, d - 1], device_id=peer
            ),
            pltpu.make_async_remote_copy(
                redw.at[g], redw.at[g], rs.at[1, d - 1], rr.at[1, d - 1], device_id=peer
            ),
        )

    for d in range(1, ngrp):
        for copy in r_copies(d):
            copy.start()
    for d in range(1, ngrp):
        for copy in r_copies(d):
            copy.wait_recv()
    for i in range(nz):
        y_copy(i).wait_send()
        gy_copy(i).wait_send()
    for i in range(nz - 1):
        z_copy(i).wait_send()
        gz_copy(i).wait_send()
    for d in range(1, ngrp):
        for copy in r_copies(d):
            copy.wait_send()


def add_groups(norm, redl, redw, lev_out, wg_out):
    total, weight = redl[0], redw[0]
    for e in range(1, redl.shape[0]):
        total = total + redl[e]
        weight = weight + redw[e]
    lev_out[...] = total * norm
    wg_out[...] = weight * norm


def local(dosages, variant_weight, block_id, stack_weight, labels):
    persons, variants = dosages.shape
    nvar, ngrp = lax.axis_size("var"), lax.axis_size("grp")
    total_preds, traits = stack_weight.shape
    kb = total_preds // nvar
    rows = labels.shape[0]
    nz = nvar // 2
    norm = 1.0 / math.sqrt(persons * ngrp)
    block = (traits, rows)
    dma = pltpu.SemaphoreType.DMA
    hbm = pl.BlockSpec(memory_space=pl.ANY)
    vmem = pl.BlockSpec(memory_space=pltpu.VMEM)
    sums = pl.pallas_call(
        functools.partial(kernel, nvar, ngrp),
        out_shape=(
            jax.ShapeDtypeStruct((ngrp, traits, kb), F32),
            jax.ShapeDtypeStruct((ngrp, 1, variants), F32),
        ),
        in_specs=[hbm] * 5,
        out_specs=(vmem, vmem),
        scratch_shapes=[
            pltpu.VMEM((variants,), BF16),
            pltpu.VMEM((variants,), jnp.int32),
            pltpu.VMEM((nvar, rows, variants), jnp.int32),
            pltpu.VMEM((nvar, rows, variants), BF16),
            pltpu.VMEM((variants, kb), BF16),
            pltpu.VMEM((kb, traits), BF16),
            pltpu.VMEM((traits, kb), BF16),
            pltpu.VMEM((traits, rows), jnp.int32),
            pltpu.VMEM((nvar, rows, kb), BF16),
            pltpu.VMEM((nz,) + block, F32),
            pltpu.VMEM((nz,) + block, F32),
            pltpu.VMEM((nz,) + block, F32),
            pltpu.VMEM((nz,) + block, F32),
            pltpu.VMEM((nz,) + block, F32),
            pltpu.VMEM((nz,) + block, BF16),
            pltpu.VMEM((nz,) + block, BF16),
            pltpu.VMEM((kb, variants), F32),
            pltpu.VMEM((traits, kb), F32),
            dma((nvar,)),
            dma((4,)),
            dma((nz,)),
            dma((nz,)),
            dma((nz,)),
            dma((nz,)),
            dma((nz,)),
            dma((nz,)),
            dma((nz,)),
            dma((nz,)),
            dma((2, ngrp - 1)),
            dma((2, ngrp - 1)),
        ],
        compiler_params=pltpu.CompilerParams(
            collective_id=0, has_side_effects=True, vmem_limit_bytes=60 * 1024 * 1024
        ),
    )(dosages, variant_weight, block_id, stack_weight.T, labels.T)
    level, weight = pl.pallas_call(
        functools.partial(add_groups, norm),
        out_shape=(
            jax.ShapeDtypeStruct((traits, kb), F32),
            jax.ShapeDtypeStruct((1, variants), F32),
        ),
        in_specs=[vmem, vmem],
        out_specs=(vmem, vmem),
    )(*sums)
    return level.T, weight.reshape(variants)


def solution(mesh):
    return jax.shard_map(
        local,
        mesh=mesh,
        in_specs=(P("grp", "var"), P("var"), P("var"), P(), P(("grp", "var"), None)),
        out_specs=(P("var", None), P("var")),
        check_vma=False,
    )
```

```python
import functools
import math

import jax
import jax.numpy as jnp
from jax import lax
from jax.experimental import pallas as pl
from jax.experimental.pallas import tpu as pltpu
from jax.sharding import PartitionSpec as P

F32, BF16 = jnp.float32, jnp.bfloat16


def flip(a, k, count):
    total, bit = 0, 1
    while bit < count:
        total = total + bit * ((a // bit + k // bit) % 2)
        bit *= 2
    return total


def zeros_below(k, bits):
    count = 0
    while count < bits and k % (1 << (count + 1)) == 0:
        count += 1
    return count


def kernel(
    nvar, ngrp, cuts, window, dos, wt_hbm, bid_hbm, sw, lab, redl, redw,
    wt, bid, dint, dose, wmat, wback, wown, labv, pred, part, own, yrecv, zrecv, gathz, gathy,
    colacc, levacc,
    dsem, csem, ys, yr, zs, zr, gzs, gzr, gys, gyr, rs, rr,
):
    nz = nvar // 2
    bits = nz.bit_length() - 1
    half = cuts * nz
    traits, sub = part.shape[1:]
    kb = wown.shape[1]
    v = lax.axis_index("var")
    g = lax.axis_index("grp")
    z, y = v // 2, v % 2
    partner = z * 2 + (1 - y)

    def piece(k, parity, h):
        return (flip(z, k, nz) * 2 + parity) * cuts + h

    def place(s):
        late = s // half
        q, t = s, s - half
        h = (1 - late) * (q // nz) + late * (t % cuts)
        i = (1 - late) * (q % nz) + late * (t // cuts)
        return piece(nz - 1 - i, y * late + (1 - y) * (1 - late), h)

    def dose_copy(s):
        start = pl.multiple_of(place(s) * sub, sub)
        return pltpu.make_async_copy(dos.at[pl.ds(start, sub)], dint.at[s], dsem.at[s])

    wt_copy = pltpu.make_async_copy(wt_hbm, wt, csem.at[2])
    bid_copy = pltpu.make_async_copy(bid_hbm, bid, csem.at[3])
    sw_copy = pltpu.make_async_copy(
        sw.at[:, pl.ds(pl.multiple_of(v * kb, kb), kb)], wown, csem.at[0]
    )
    lab_copy = pltpu.make_async_copy(lab, labv, csem.at[1])
    wt_copy.start()
    bid_copy.start()
    sw_copy.start()
    for s in range(window):
        dose_copy(s).start()
    lab_copy.start()

    barrier = pltpu.get_barrier_semaphore()
    pl.semaphore_signal(barrier, inc=1, device_id={"var": partner})
    for r in range(bits):
        pl.semaphore_signal(barrier, inc=1, device_id={"var": flip(z, 1 << r, nz) * 2 + y})
    for d in range(1, ngrp):
        pl.semaphore_signal(barrier, inc=1, device_id={"grp": (g + d) % ngrp})

    wt_copy.wait()
    bid_copy.wait()
    hot = lax.broadcasted_iota(jnp.int32, (kb, wt.shape[0]), 0) == bid[...][None, :]
    wmat[...] = jnp.where(hot, wt[...].astype(F32)[None, :], 0.0).T.astype(BF16)
    sw_copy.wait()
    wback[...] = wown[...].astype(F32).T.astype(BF16)
    colacc[...] = jnp.zeros_like(colacc)
    levacc[...] = jnp.zeros_like(levacc)

    def forward(s):
        dose_copy(s).wait()
        ahead = s + window
        if isinstance(s, int):
            if ahead < 2 * half:
                dose_copy(ahead).start()
        else:

            @pl.when(ahead < 2 * half)
            def _():
                dose_copy(ahead).start()

        at = place(s)
        d = dint[s].astype(F32).astype(BF16)
        dose[at] = d
        p = jnp.dot(d, wmat[...], preferred_element_type=F32).astype(BF16)
        pred[at] = p
        return lax.dot_general(
            wown[...], p, (((1,), (1,)), ((), ())), preferred_element_type=F32
        )

    def remote(src, dst, send, recv, peer):
        return pltpu.make_async_remote_copy(src, dst, send, recv, device_id={"var": peer})

    def across(r):
        return flip(z, 1 << r, nz) * 2 + y

    def y_copy(q):
        return remote(part.at[q], yrecv.at[q], ys.at[q], yr.at[q], partner)

    def z_copy(h, k):
        q = h * nz + nz - 1 - k
        peer = across(zeros_below(k, bits))
        return remote(own.at[q], zrecv.at[q], zs.at[q], zr.at[q], peer)

    def gz_copy(h, k):
        r = zeros_below(k, bits)
        q, src = h * nz + k, h * nz + k - (1 << r)
        return remote(gathz.at[src], gathz.at[q], gzs.at[q], gzr.at[q], across(r))

    def gy_copy(q):
        return remote(gathz.at[q], gathy.at[q], gys.at[q], gyr.at[q], partner)

    part[0] = forward(0)
    pl.semaphore_wait(barrier, bits + ngrp)
    y_copy(0).start()

    def first(s, carry):
        part[s] = forward(s)
        y_copy(s).start()
        return carry

    lax.fori_loop(1, half, first, 0)

    def reduce_step(h, k):
        q = h * nz + nz - 1 - k
        y_copy(q).wait_recv()
        total = own[q] + yrecv[q]
        for r in range(zeros_below(k, bits) if k else bits):
            other = k + (1 << r)
            z_copy(h, other).wait_recv()
            total = total + zrecv[h * nz + nz - 1 - other]
        if k:
            own[q] = total
            z_copy(h, k).start()
            return
        target = labv[:, h * sub : (h + 1) * sub].astype(F32)
        gathz[h * nz] = (jax.nn.sigmoid(total) - target).astype(BF16)
        send_on(h, 0)

    def send_on(h, k):
        for r in reversed(range(zeros_below(k, bits) if k else bits)):
            gz_copy(h, k + (1 << r)).start()
        gy_copy(h * nz + k).start()

    def backward(resid, at):
        lg = jnp.dot(wback[...], resid, preferred_element_type=F32).astype(BF16)
        colacc[...] += jnp.dot(lg, dose[at], preferred_element_type=F32)
        levacc[...] += jnp.dot(resid, pred[at], preferred_element_type=F32)

    def gather_step(h, k):
        gz_copy(h, k).wait_recv()
        send_on(h, k)

    order = sorted(range(1, nz), key=lambda k: (-zeros_below(k, bits), k))

    lab_copy.wait()
    for i in range(nz):
        for h in range(cuts):
            own[h * nz + i] = forward(half + i * cuts + h)
        if i < nz - 1:
            reduce_step(0, nz - 1 - i)
    for h in range(cuts):
        if h + 1 < cuts:
            reduce_step(h + 1, nz - 1)
        reduce_step(h, 0)
        if h + 1 < cuts:
            for k in range(nz - 2, 0, -1):
                reduce_step(h + 1, k)
        else:
            for k in order:
                gather_step(h, k)
        if h + 1 < cuts:
            for k in order:
                gather_step(h, k)

    def near(q, carry):
        backward(gathz[q], piece(q % nz, y, q // nz))
        return carry

    def far(q, carry):
        gy_copy(q).wait_recv()
        backward(gathy[q], piece(q % nz, 1 - y, q // nz))
        return carry

    for h in range(cuts):
        lax.fori_loop(h * nz, (h + 1) * nz, near, 0)
        lax.fori_loop(h * nz, (h + 1) * nz, far, 0)

    hot = lax.broadcasted_iota(jnp.int32, colacc.shape, 0) == bid[...][None, :]
    redw[g] = jnp.sum(jnp.where(hot, colacc[...], 0.0), axis=0, keepdims=True)
    redl[g] = levacc[...]

    def r_copies(d):
        peer = {"grp": (g + d) % ngrp}
        return (
            pltpu.make_async_remote_copy(
                redl.at[g], redl.at[g], rs.at[0, d - 1], rr.at[0, d - 1], device_id=peer
            ),
            pltpu.make_async_remote_copy(
                redw.at[g], redw.at[g], rs.at[1, d - 1], rr.at[1, d - 1], device_id=peer
            ),
        )

    for d in range(1, ngrp):
        for copy in r_copies(d):
            copy.start()
    for h in range(cuts):
        for k in range(nz):
            y_copy(h * nz + k).wait_send()
            gy_copy(h * nz + k).wait_send()
            if k:
                z_copy(h, k).wait_send()
                gz_copy(h, k).wait_send()
    for d in range(1, ngrp):
        for copy in r_copies(d):
            copy.wait_send()
            copy.wait_recv()


def add_groups(norm, redl, redw, lev_out, wg_out):
    total, weight = redl[0], redw[0]
    for e in range(1, redl.shape[0]):
        total = total + redl[e]
        weight = weight + redw[e]
    lev_out[...] = total * norm
    wg_out[...] = weight * norm


def local(dosages, variant_weight, block_id, stack_weight, labels):
    persons, variants = dosages.shape
    nvar, ngrp = lax.axis_size("var"), lax.axis_size("grp")
    total_preds, traits = stack_weight.shape
    kb = total_preds // nvar
    rows = labels.shape[0]
    cuts = 2 if rows % 256 == 0 else 1
    sub, count = rows // cuts, cuts * nvar // 2
    norm = 1.0 / math.sqrt(persons * ngrp)
    block = (count, traits, sub)
    dma = pltpu.SemaphoreType.DMA
    hbm = pl.BlockSpec(memory_space=pl.ANY)
    vmem = pl.BlockSpec(memory_space=pltpu.VMEM)
    sums = pl.pallas_call(
        functools.partial(kernel, nvar, ngrp, cuts, min(6, cuts * nvar)),
        out_shape=(
            jax.ShapeDtypeStruct((ngrp, traits, kb), F32),
            jax.ShapeDtypeStruct((ngrp, 1, variants), F32),
        ),
        in_specs=[hbm] * 5,
        out_specs=(vmem, vmem),
        scratch_shapes=[
            pltpu.VMEM((variants,), BF16),
            pltpu.VMEM((variants,), jnp.int32),
            pltpu.VMEM((2 * count, sub, variants), jnp.int32),
            pltpu.VMEM((2 * count, sub, variants), BF16),
            pltpu.VMEM((variants, kb), BF16),
            pltpu.VMEM((kb, traits), BF16),
            pltpu.VMEM((traits, kb), BF16),
            pltpu.VMEM((traits, rows), jnp.int32),
            pltpu.VMEM((2 * count, sub, kb), BF16),
            pltpu.VMEM(block, F32),
            pltpu.VMEM(block, F32),
            pltpu.VMEM(block, F32),
            pltpu.VMEM(block, F32),
            pltpu.VMEM(block, BF16),
            pltpu.VMEM(block, BF16),
            pltpu.VMEM((kb, variants), F32),
            pltpu.VMEM((traits, kb), F32),
            dma((2 * count,)),
            dma((4,)),
            dma((count,)),
            dma((count,)),
            dma((count,)),
            dma((count,)),
            dma((count,)),
            dma((count,)),
            dma((count,)),
            dma((count,)),
            dma((2, ngrp - 1)),
            dma((2, ngrp - 1)),
        ],
        compiler_params=pltpu.CompilerParams(
            collective_id=0, has_side_effects=True, vmem_limit_bytes=60 * 1024 * 1024
        ),
    )(dosages, variant_weight, block_id, stack_weight.T, labels.T)
    level, weight = pl.pallas_call(
        functools.partial(add_groups, norm),
        out_shape=(
            jax.ShapeDtypeStruct((traits, kb), F32),
            jax.ShapeDtypeStruct((1, variants), F32),
        ),
        in_specs=[vmem, vmem],
        out_specs=(vmem, vmem),
    )(*sums)
    return level.T, weight.reshape(variants)


def solution(mesh):
    return jax.shard_map(
        local,
        mesh=mesh,
        in_specs=(P("grp", "var"), P("var"), P("var"), P(), P(("grp", "var"), None)),
        out_specs=(P("var", None), P("var")),
        check_vma=False,
    )
```

```python
import functools
import math

import jax
import jax.numpy as jnp
from jax import lax
from jax.experimental import pallas as pl
from jax.experimental.pallas import tpu as pltpu
from jax.sharding import PartitionSpec as P

F32, BF16 = jnp.float32, jnp.bfloat16


def flip(a, k, count):
    total, bit = 0, 1
    while bit < count:
        total = total + bit * ((a // bit + k // bit) % 2)
        bit *= 2
    return total


def zeros_below(k, bits):
    count = 0
    while count < bits and k % (1 << (count + 1)) == 0:
        count += 1
    return count


def kernel(
    nvar, ngrp, cuts, window, dos, wt_hbm, bid_hbm, sw, lab, redl, redw,
    wt, bid, dint, dose, wmat, wback, wown, labv, pred, part, own, yrecv, zrecv, gathz, gathy,
    colacc, levacc,
    dsem, csem, ys, yr, zs, zr, gzs, gzr, gys, gyr, rs, rr,
):
    nz = nvar // 2
    bits = nz.bit_length() - 1
    half = cuts * nz
    flight = 2
    traits, sub = part.shape[1:]
    kb = wown.shape[1]
    v = lax.axis_index("var")
    g = lax.axis_index("grp")
    z, y = v // 2, v % 2
    partner = z * 2 + (1 - y)

    def piece(k, parity, h):
        return (flip(z, k, nz) * 2 + parity) * cuts + h

    def place(s):
        late = s // half
        q, t = s, s - half
        h = (1 - late) * (q // nz) + late * (t % cuts)
        i = (1 - late) * (q % nz) + late * (t // cuts)
        return piece(nz - 1 - i, y * late + (1 - y) * (1 - late), h)

    def dose_copy(s):
        start = pl.multiple_of(place(s) * sub, sub)
        return pltpu.make_async_copy(dos.at[pl.ds(start, sub)], dint.at[s], dsem.at[s])

    wt_copy = pltpu.make_async_copy(wt_hbm, wt, csem.at[2])
    bid_copy = pltpu.make_async_copy(bid_hbm, bid, csem.at[3])
    sw_copy = pltpu.make_async_copy(
        sw.at[:, pl.ds(pl.multiple_of(v * kb, kb), kb)], wown, csem.at[0]
    )
    lab_copy = pltpu.make_async_copy(lab, labv, csem.at[1])
    wt_copy.start()
    bid_copy.start()
    sw_copy.start()
    for s in range(window):
        dose_copy(s).start()
    lab_copy.start()

    barrier = pltpu.get_barrier_semaphore()
    pl.semaphore_signal(barrier, inc=1, device_id={"var": partner})
    for r in range(bits):
        pl.semaphore_signal(barrier, inc=1, device_id={"var": flip(z, 1 << r, nz) * 2 + y})
    for d in range(1, ngrp):
        pl.semaphore_signal(barrier, inc=1, device_id={"grp": (g + d) % ngrp})

    wt_copy.wait()
    bid_copy.wait()
    hot = lax.broadcasted_iota(jnp.int32, (kb, wt.shape[0]), 0) == bid[...][None, :]
    wmat[...] = jnp.where(hot, wt[...].astype(F32)[None, :], 0.0).T.astype(BF16)
    sw_copy.wait()
    wback[...] = wown[...].astype(F32).T.astype(BF16)
    colacc[...] = jnp.zeros_like(colacc)
    levacc[...] = jnp.zeros_like(levacc)

    def forward(s):
        dose_copy(s).wait()
        ahead = s + window
        if isinstance(s, int):
            if ahead < 2 * half:
                dose_copy(ahead).start()
        else:

            @pl.when(ahead < 2 * half)
            def _():
                dose_copy(ahead).start()

        at = place(s)
        d = dint[s].astype(F32).astype(BF16)
        dose[at] = d
        p = jnp.dot(d, wmat[...], preferred_element_type=F32).astype(BF16)
        pred[at] = p
        return lax.dot_general(
            wown[...], p, (((1,), (1,)), ((), ())), preferred_element_type=F32
        )

    def remote(src, dst, send, recv, peer):
        return pltpu.make_async_remote_copy(src, dst, send, recv, device_id={"var": peer})

    def across(r):
        return flip(z, 1 << r, nz) * 2 + y

    def y_copy(q):
        return remote(part.at[q], yrecv.at[q], ys.at[q], yr.at[q], partner)

    def z_copy(h, k):
        q = h * nz + nz - 1 - k
        peer = across(zeros_below(k, bits))
        return remote(own.at[q], zrecv.at[q], zs.at[q], zr.at[q], peer)

    def gz_copy(h, k):
        r = zeros_below(k, bits)
        q, src = h * nz + k, h * nz + k - (1 << r)
        return remote(gathz.at[src], gathz.at[q], gzs.at[q], gzr.at[q], across(r))

    def gy_copy(q):
        return remote(gathz.at[q], gathy.at[q], gys.at[q], gyr.at[q], partner)

    part[0] = forward(0)
    pl.semaphore_wait(barrier, bits + ngrp)
    y_copy(0).start()

    def first(s, carry):
        part[s] = forward(s)

        @pl.when(s < flight)
        def _():
            y_copy(s).start()

        return carry

    lax.fori_loop(1, half, first, 0)
    started = [min(flight, half)]

    def reduce_step(h, k):
        q = h * nz + nz - 1 - k
        y_copy(q).wait_recv()
        if started[0] < half:
            y_copy(started[0]).start()
            started[0] += 1
        total = own[q] + yrecv[q]
        for r in range(zeros_below(k, bits) if k else bits):
            other = k + (1 << r)
            z_copy(h, other).wait_recv()
            total = total + zrecv[h * nz + nz - 1 - other]
        if k:
            own[q] = total
            z_copy(h, k).start()
            return
        target = labv[:, h * sub : (h + 1) * sub].astype(F32)
        gathz[h * nz] = (jax.nn.sigmoid(total) - target).astype(BF16)
        send_on(h, 0)

    def send_on(h, k):
        for r in reversed(range(zeros_below(k, bits) if k else bits)):
            gz_copy(h, k + (1 << r)).start()
        gy_copy(h * nz + k).start()

    def backward(resid, at):
        lg = jnp.dot(wback[...], resid, preferred_element_type=F32).astype(BF16)
        colacc[...] += jnp.dot(lg, dose[at], preferred_element_type=F32)
        levacc[...] += jnp.dot(resid, pred[at], preferred_element_type=F32)

    def gather_step(h, k):
        gz_copy(h, k).wait_recv()
        send_on(h, k)

    def near(q, carry):
        backward(gathz[q], piece(q % nz, y, q // nz))
        return carry

    def far(q, carry):
        gy_copy(q).wait_recv()
        backward(gathy[q], piece(q % nz, 1 - y, q // nz))
        return carry

    order = sorted(range(1, nz), key=lambda k: (-zeros_below(k, bits), k))

    lab_copy.wait()
    for i in range(nz):
        for h in range(cuts):
            own[h * nz + i] = forward(half + i * cuts + h)
        if i < nz - 1:
            reduce_step(0, nz - 1 - i)
    for h in range(cuts):
        if h + 1 < cuts:
            reduce_step(h + 1, nz - 1)
        reduce_step(h, 0)
        if h + 1 < cuts:
            for k in range(nz - 2, 0, -1):
                reduce_step(h + 1, k)
            for k in order:
                gather_step(h, k)
        else:
            if h:
                lax.fori_loop(0, h * nz, near, 0)
            for k in order:
                gather_step(h, k)
    if cuts > 1:
        lax.fori_loop(0, half - nz, far, 0)
    lax.fori_loop(half - nz, half, near, 0)
    lax.fori_loop(half - nz, half, far, 0)

    hot = lax.broadcasted_iota(jnp.int32, colacc.shape, 0) == bid[...][None, :]
    redw[g] = jnp.sum(jnp.where(hot, colacc[...], 0.0), axis=0, keepdims=True)
    redl[g] = levacc[...]

    def r_copies(d):
        peer = {"grp": (g + d) % ngrp}
        return (
            pltpu.make_async_remote_copy(
                redl.at[g], redl.at[g], rs.at[0, d - 1], rr.at[0, d - 1], device_id=peer
            ),
            pltpu.make_async_remote_copy(
                redw.at[g], redw.at[g], rs.at[1, d - 1], rr.at[1, d - 1], device_id=peer
            ),
        )

    for d in range(1, ngrp):
        for copy in r_copies(d):
            copy.start()
    for h in range(cuts):
        for k in range(nz):
            y_copy(h * nz + k).wait_send()
            gy_copy(h * nz + k).wait_send()
            if k:
                z_copy(h, k).wait_send()
                gz_copy(h, k).wait_send()
    for d in range(1, ngrp):
        for copy in r_copies(d):
            copy.wait_send()
            copy.wait_recv()


def add_groups(norm, redl, redw, lev_out, wg_out):
    total, weight = redl[0], redw[0]
    for e in range(1, redl.shape[0]):
        total = total + redl[e]
        weight = weight + redw[e]
    lev_out[...] = total * norm
    wg_out[...] = weight * norm


def local(dosages, variant_weight, block_id, stack_weight, labels):
    persons, variants = dosages.shape
    nvar, ngrp = lax.axis_size("var"), lax.axis_size("grp")
    total_preds, traits = stack_weight.shape
    kb = total_preds // nvar
    rows = labels.shape[0]
    cuts = 1
    sub, count = rows // cuts, cuts * nvar // 2
    norm = 1.0 / math.sqrt(persons * ngrp)
    block = (count, traits, sub)
    dma = pltpu.SemaphoreType.DMA
    hbm = pl.BlockSpec(memory_space=pl.ANY)
    vmem = pl.BlockSpec(memory_space=pltpu.VMEM)
    sums = pl.pallas_call(
        functools.partial(kernel, nvar, ngrp, cuts, min(3, cuts * nvar)),
        out_shape=(
            jax.ShapeDtypeStruct((ngrp, traits, kb), F32),
            jax.ShapeDtypeStruct((ngrp, 1, variants), F32),
        ),
        in_specs=[hbm] * 5,
        out_specs=(vmem, vmem),
        scratch_shapes=[
            pltpu.VMEM((variants,), BF16),
            pltpu.VMEM((variants,), jnp.int32),
            pltpu.VMEM((2 * count, sub, variants), jnp.int32),
            pltpu.VMEM((2 * count, sub, variants), BF16),
            pltpu.VMEM((variants, kb), BF16),
            pltpu.VMEM((kb, traits), BF16),
            pltpu.VMEM((traits, kb), BF16),
            pltpu.VMEM((traits, rows), jnp.int32),
            pltpu.VMEM((2 * count, sub, kb), BF16),
            pltpu.VMEM(block, F32),
            pltpu.VMEM(block, F32),
            pltpu.VMEM(block, F32),
            pltpu.VMEM(block, F32),
            pltpu.VMEM(block, BF16),
            pltpu.VMEM(block, BF16),
            pltpu.VMEM((kb, variants), F32),
            pltpu.VMEM((traits, kb), F32),
            dma((2 * count,)),
            dma((4,)),
            dma((count,)),
            dma((count,)),
            dma((count,)),
            dma((count,)),
            dma((count,)),
            dma((count,)),
            dma((count,)),
            dma((count,)),
            dma((2, ngrp - 1)),
            dma((2, ngrp - 1)),
        ],
        compiler_params=pltpu.CompilerParams(
            collective_id=0, has_side_effects=True, vmem_limit_bytes=60 * 1024 * 1024
        ),
    )(dosages, variant_weight, block_id, stack_weight.T, labels.T)
    level, weight = pl.pallas_call(
        functools.partial(add_groups, norm),
        out_shape=(
            jax.ShapeDtypeStruct((traits, kb), F32),
            jax.ShapeDtypeStruct((1, variants), F32),
        ),
        in_specs=[vmem, vmem],
        out_specs=(vmem, vmem),
    )(*sums)
    return level.T, weight.reshape(variants)


def solution(mesh):
    return jax.shard_map(
        local,
        mesh=mesh,
        in_specs=(P("grp", "var"), P("var"), P("var"), P(), P(("grp", "var"), None)),
        out_specs=(P("var", None), P("var")),
        check_vma=False,
    )
```
